32 devices in a mesh: mem: 8 (over z, core), ma: 4 (over y, x).
Axes of the slice: x: 2, y: 2, z: 4, core: 2. Of those that a mesh axis runs over, the one named last changes fastest.
Arguments:
- ar_state: float32 [3, 32, 128, 2, 1280], P(None, 'mem', 'ma'), may hold values from -4 to 4
- forcing: float32 [3, 32, 128, 2, 1280], P(None, 'mem', 'ma'), may hold values from -6 to 6
- ar_decay: float32 [3], replicated, may hold values from 0.3 to 0.95
- amplitude: float32 [3, 1280], replicated, may hold values from 0.05 to 0.4
- wavenumber: int32 [128], replicated, may hold values from 0 to 1279, as said below
- tables: bfloat16 [128, 1280, 320], P('ma', None, 'mem'), may hold values from -0.15625 to 0.15625
- tendencies: bfloat16 [32, 320, 5120], P('mem', 'ma'), may hold values from -6 to 6
Outputs:
- perturbed: bfloat16 [32, 320, 5120], P('mem', 'ma')
- new_state: float32 [3, 32, 128, 2, 1280], P(None, 'mem', 'ma')
The draws below stay inside these ranges and needn't reach their ends.
Inputs may be any that keep to these rules, and one draw needn't show every extreme that they name: `wavenumber`: 128 distinct values.
All inputs are finite; a program needn't handle non-finite values.
Results may differ from the reference program's by a relative error of at most 0.0042.
Values may be sent and summed in bfloat16 or wider, within the bound.
A program may use at most 64 MiB of HBM per device.

```python
import math
import jax
import jax.numpy as jnp
from jax import lax

MWIN = 128
NDEG = 1280
NLON = 5120
SCALES = 3
MEMBERS = 32
NLAT = 320


def draw_wavenumber(key, part):
    return jax.random.permutation(key, NDEG)[:MWIN].astype(jnp.int32)


def steps_of(rng, extent, shards, low, largest):
    loudness, own = 1.0, jax.random.fold_in(rng, 6)
    for axis_at, shards_of in shards:
        draws = jnp.exp(jax.random.uniform(jax.random.fold_in(own, axis_at), (shards_of,), jnp.float32, low / len(shards), largest / len(shards)))
        loudness = loudness * jnp.repeat(draws, extent[axis_at] // shards_of).reshape([-1 if axis == axis_at else 1 for axis in range(len(extent))])
    return loudness


def scatter_about(rng, shape, scale, most, pieces=(), kind=jnp.bfloat16):
    values = scale * jax.random.normal(rng, shape, jnp.float32)
    if pieces:
        values = values * steps_of(rng, shape, pieces, -0.22, 0.18)
    return jnp.clip(values, -most, most).astype(kind)


def setup_inputs(seed: int = 0) -> dict:
    streams_of = jax.random.split(jax.random.key(seed), 8)
    return {
        "ar_state": scatter_about(streams_of[0], (SCALES, MEMBERS, MWIN, 2, NDEG), 0.5, 4.0, ((1, 8), (2, 4)), jnp.float32),
        "forcing": scatter_about(streams_of[1], (SCALES, MEMBERS, MWIN, 2, NDEG), 1.0, 6.0, ((1, 8), (2, 4)), jnp.float32),
        "ar_decay": jnp.clip(jnp.exp(jax.random.uniform(streams_of[2], (SCALES,), jnp.float32, math.log(0.3), math.log(0.95))), 0.3, 0.95),
        "amplitude": jnp.clip(jnp.exp(jax.random.uniform(streams_of[3], (SCALES, NDEG), jnp.float32, math.log(0.05), math.log(0.4))), 0.05, 0.4),
        "wavenumber": draw_wavenumber(jax.random.fold_in(streams_of[7], 71), 0),
        "tables": scatter_about(streams_of[5], (MWIN, NDEG, NLAT), NDEG ** -0.5, 0.15625, ((0, 4), (2, 8))),
        "tendencies": scatter_about(streams_of[6], (MEMBERS, NLAT, NLON), 1.0, 6.0, ((0, 8), (1, 4))),
    }


clip_level = 0.9

def basis_table(wavenumber, lon_count):
    longitude = lax.broadcasted_iota(jnp.int32, (wavenumber.shape[0], lon_count), 1)
    phases = wavenumber[:, None] * longitude % lon_count
    angles = phases.astype(jnp.float32) * (2.0 * math.pi / lon_count)
    stacked = jnp.stack([jnp.cos(angles), -jnp.sin(angles)], axis=1)
    return stacked.reshape(2 * wavenumber.shape[0], lon_count).astype(jnp.bfloat16)

def reference(ar_state, forcing, ar_decay, amplitude, wavenumber, tables, tendencies):
    degree_grid = lax.broadcasted_iota(jnp.int32, (MWIN, NDEG), 1)
    kept_mask = (degree_grid >= wavenumber[:, None]).astype(jnp.float32)
    updated = ar_decay[:, None, None, None, None] * ar_state + amplitude[:, None, None, None, :] * forcing
    new_state = kept_mask[None, None, :, None, :] * updated
    coefficients = lax.optimization_barrier(jnp.sum(new_state, axis=0)).astype(jnp.bfloat16)

    def per_wave(index):
        block_rows = lax.dynamic_index_in_dim(coefficients, index, 1, keepdims=False)
        wave_table = lax.dynamic_index_in_dim(tables, index, 0, keepdims=False)
        product = jnp.dot(block_rows.reshape(2 * MEMBERS, NDEG), wave_table, preferred_element_type=jnp.float32)
        return product.reshape(MEMBERS, 2, NLAT)
    fourier = lax.map(per_wave, jnp.arange(MWIN, dtype=jnp.int32))
    fourier = jnp.transpose(fourier, (1, 3, 0, 2)).astype(jnp.bfloat16)
    basis = basis_table(wavenumber, NLON)

    def per_member(pair):
        member_rows, member_tend = pair
        pattern = jnp.dot(member_rows.reshape(NLAT, 2 * MWIN), basis, preferred_element_type=jnp.float32)
        pattern = jnp.clip(pattern * (1.0 / math.sqrt(MWIN)), -clip_level, clip_level)
        return (member_tend.astype(jnp.float32) * (1.0 + pattern)).astype(jnp.bfloat16)
    perturbed = lax.map(per_member, (fourier, tendencies))
    return (perturbed, new_state)
```

```python
import functools
import math

import jax
import jax.numpy as jnp
from jax import lax
from jax.experimental import pallas as pl
from jax.experimental.pallas import tpu as pltpu
from jax.sharding import PartitionSpec as P

clip_level = 0.9
MESH = pl.DeviceIdType.MESH
PACK = 4


def legendre_kernel(N, M, c_ref, t_hbm, o_ref, gath, tabs, prod, send, land,
                    tsem, lsem, ssem, rsem, s1, r1, s2, r2):
    Z = N // 2
    Q = c_ref.shape[0]
    L = tabs.shape[1] // PACK
    R = N // M
    me = lax.axis_index("mem")
    mk = lax.axis_index("ma")
    z, p = lax.div(me, 2), lax.rem(me, 2)
    mate = z * 2 + 1 - p

    barrier = pltpu.get_barrier_semaphore()
    for d in range(1, N):
        pl.semaphore_signal(barrier, inc=1, device_id={"mem": lax.rem(me + d, N)}, device_id_type=MESH)
    for d in range(1, M):
        pl.semaphore_signal(barrier, inc=1, device_id={"ma": lax.rem(mk + d, M)}, device_id_type=MESH)

    def table_copy(q):
        return pltpu.make_async_copy(t_hbm.at[q], tabs.at[q], tsem.at[q])

    def own_copy(q):
        return pltpu.make_async_copy(c_ref.at[q], gath.at[q, me], lsem.at[q])

    def hop(way, q, src, ref, dst):
        return pltpu.make_async_remote_copy(
            src_ref=ref, dst_ref=gath.at[q, src], send_sem=ssem.at[way, q, src],
            recv_sem=rsem.at[q, src], device_id={"mem": dst}, device_id_type=MESH)

    pl.semaphore_wait(barrier, N - 1 + M - 1)

    @pl.loop(0, Q)
    def _(q):
        @pl.when(z + 1 < Z)
        def _():
            hop(0, q, me, c_ref.at[q], me + 2).start()

        @pl.when(z > 0)
        def _():
            hop(1, q, me, c_ref.at[q], me - 2).start()

        hop(2, q, me, c_ref.at[q], mate).start()
        own_copy(q).start()
        table_copy(q).start()

    def arrived(q, src):
        hop(2, q, src, gath.at[q, src], mate).wait_recv()

    def relay(q, src, way, more, dst):
        arrived(q, src)

        @pl.when(more)
        def _():
            hop(way, q, src, gath.at[q, src], dst).start()

        hop(2, q, src, gath.at[q, src], mate).start()

    @pl.loop(0, Q + Z - 2)
    def _(s):
        for h in range(1, Z):
            q = s - h + 1
            live = jnp.logical_and(q >= 0, q < Q)

            @pl.when(jnp.logical_and(live, z - h >= 0))
            def _():
                relay(q, me - 2 * h, 0, z + 1 < Z, me + 2)

            @pl.when(jnp.logical_and(live, z + h < Z))
            def _():
                relay(q, me + 2 * h, 1, z > 0, me - 2)

        q = s - (Z - 2)

        @pl.when(q >= 0)
        def _():
            own_copy(q).wait()
            table_copy(q).wait()
            for i in range(Z):
                arrived(q, 2 * i + 1 - p)
            lhs = gath[q].reshape(-1, gath.shape[3])
            full = lax.dot_general(lhs, tabs[q], (((1,), (1,)), ((), ())), preferred_element_type=jnp.float32)
            slot = lax.broadcasted_iota(jnp.int32, (full.shape[0], L), 0) % (2 * PACK) // 2
            diag = full[:, :L]
            for j in range(1, PACK):
                diag = jnp.where(slot == j, full[:, j * L:(j + 1) * L], diag)
            prod[:, :, q] = diag.reshape(prod.shape[0], prod.shape[1], 2 * PACK, L)

    H = send.shape[1]

    def out1(dst):
        return pltpu.make_async_remote_copy(
            src_ref=send.at[dst], dst_ref=land.at[me], send_sem=s1.at[dst],
            recv_sem=r1.at[me], device_id={"mem": dst}, device_id_type=MESH)

    def in1(src):
        return pltpu.make_async_remote_copy(
            src_ref=send.at[src], dst_ref=land.at[src], send_sem=s1.at[src],
            recv_sem=r1.at[src], device_id={"mem": src}, device_id_type=MESH)

    @pl.loop(1, N)
    def _(d):
        dst = lax.rem(me + d, N)
        for h in range(H):
            block = prod[dst * H + h].reshape(-1, L)
            send[dst, h] = block.T.astype(jnp.bfloat16)
        out1(dst).start()

    for h in range(H):
        block = prod[me * H + h].reshape(-1, L)
        land[me, h] = block.T.astype(jnp.bfloat16)

    def out2(kk):
        return pltpu.make_async_remote_copy(
            src_ref=land.at[pl.ds(R * kk, R)], dst_ref=o_ref.at[mk], send_sem=s2.at[kk],
            recv_sem=r2.at[mk], device_id={"ma": kk}, device_id_type=MESH)

    def in2(kk):
        return pltpu.make_async_remote_copy(
            src_ref=land.at[pl.ds(R * kk, R)], dst_ref=o_ref.at[kk], send_sem=s2.at[kk],
            recv_sem=r2.at[kk], device_id={"ma": kk}, device_id_type=MESH)

    def gather_rows(kk):
        for r in range(R):
            src = R * kk + r

            @pl.when(src != me)
            def _():
                in1(src).wait_recv()

    for d in range(1, M):
        kk = lax.rem(mk + d, M)
        gather_rows(kk)
        out2(kk).start()
    gather_rows(mk)
    o_ref[mk] = land[pl.ds(R * mk, R)]
    for d in range(1, M):
        in2(lax.rem(mk + d, M)).wait_recv()

    for d in range(1, M):
        out2(lax.rem(mk + d, M)).wait_send()

    @pl.loop(1, N)
    def _(d):
        out1(lax.rem(me + d, N)).wait_send()

    @pl.loop(0, Q)
    def _(q):
        for i in range(Z):
            src = 2 * i + p
            ref = gath.at[q, src]

            @pl.when(jnp.logical_and(z + 1 < Z, z >= i))
            def _():
                hop(0, q, src, ref, me + 2).wait_send()

            @pl.when(jnp.logical_and(z > 0, z <= i))
            def _():
                hop(1, q, src, ref, me - 2).wait_send()

            hop(2, q, src, ref, mate).wait_send()


def synth_kernel(scale, f_ref, u_ref, v_ref, cb_ref, sb_ref, t_ref, o_ref, lhs, basis):
    step = pl.program_id(0)
    M, R, H, L, W = f_ref.shape
    half = W // 2

    @pl.when(step == 0)
    def _():
        parts = []
        for b in range(2 * H):
            for r in range(R):
                lo = (b % 2) * half
                row = [f_ref[k, r, b // 2].astype(jnp.float32)[:, lo:lo + half] for k in range(M)]
                parts.append(jnp.concatenate(row, axis=1))
        lhs[...] = (jnp.concatenate(parts, axis=0) * scale).astype(jnp.bfloat16) if scale else jnp.concatenate(parts, axis=0).astype(jnp.bfloat16)

    cols = o_ref.shape[2] // 128
    width = u_ref.shape[1]
    shift = lax.rem(width - step * cols, width)
    u = pltpu.roll(u_ref[...], shift, 1)
    v = pltpu.roll(v_ref[...], shift, 1)
    cb, sb = cb_ref[...], sb_ref[...]
    for a in range(cols):
        basis[:, a * 128:(a + 1) * 128] = (u[:, a:a + 1] * cb + v[:, a:a + 1] * sb).astype(jnp.bfloat16)
    pattern = jnp.dot(lhs[...], basis[...], preferred_element_type=jnp.float32)
    pattern = pattern * (1.0 / math.sqrt(basis.shape[0] // 2))
    pattern = jnp.clip(pattern, -clip_level, clip_level).reshape(o_ref.shape)
    o_ref[...] = (t_ref[...].astype(jnp.float32) * (1.0 + pattern)).astype(jnp.bfloat16)


def trig_tables(wavenumber, lon_count):
    rows = jnp.repeat(wavenumber, 2)[:, None]
    odd = (lax.broadcasted_iota(jnp.int32, (rows.shape[0], 1), 0) % 2) == 1
    width = -(-(lon_count // 128) // 128) * 128
    unit = 2.0 * math.pi / lon_count
    coarse = lax.broadcasted_iota(jnp.int32, (1, width), 1)
    fine = lax.broadcasted_iota(jnp.int32, (1, 128), 1)
    far = (rows * 128 % lon_count * coarse % lon_count).astype(jnp.float32) * unit
    near = (rows * fine % lon_count).astype(jnp.float32) * unit
    c, s = jnp.cos(far), jnp.sin(far)
    return jnp.where(odd, -s, c), jnp.where(odd, -c, -s), jnp.cos(near), jnp.sin(near)


def per_device(N, M, ar_state, forcing, ar_decay, amplitude, wavenumber, tables, tendencies):
    members, waves = ar_state.shape[1], ar_state.shape[2]
    degrees = ar_state.shape[4]
    lats = tables.shape[2]
    Q = waves // PACK
    rows = members * 2 * PACK
    owner_index = lax.axis_index("ma")
    own_waves = lax.dynamic_slice_in_dim(wavenumber, owner_index * waves, waves)
    degree_grid = lax.broadcasted_iota(jnp.int32, (waves, degrees), 1)
    kept_mask = (degree_grid >= own_waves[:, None]).astype(jnp.float32)
    updated = (
        ar_decay[:, None, None, None, None] * ar_state + amplitude[:, None, None, None, :] * forcing
    )
    new_state = kept_mask[None, None, :, None, :] * updated
    coefficients = jnp.sum(new_state, axis=0).astype(jnp.bfloat16)
    coefficients = coefficients.reshape(members, Q, 2 * PACK, degrees).transpose(1, 0, 2, 3)
    coefficients = coefficients.reshape(Q, rows, degrees)
    turned = tables.transpose(0, 2, 1).reshape(Q, PACK * lats, degrees)

    H = members // 2
    W = 2 * Q * 2 * PACK
    R = N // M
    any_spec = pl.BlockSpec(memory_space=pl.ANY)
    vmem_spec = pl.BlockSpec(memory_space=pltpu.VMEM)
    fourier = pl.pallas_call(
        functools.partial(legendre_kernel, N, M),
        out_shape=jax.ShapeDtypeStruct((M, R, H, lats, W), jnp.bfloat16),
        in_specs=[vmem_spec, any_spec],
        out_specs=vmem_spec,
        scratch_shapes=[
            pltpu.VMEM((Q, N, rows, degrees), jnp.bfloat16),
            pltpu.VMEM((Q, PACK * lats, degrees), jnp.bfloat16),
            pltpu.VMEM((N * H, 2, Q, 2 * PACK, lats), jnp.float32),
            pltpu.VMEM((N, H, lats, W), jnp.bfloat16),
            pltpu.VMEM((N, H, lats, W), jnp.bfloat16),
            pltpu.SemaphoreType.DMA((Q,)),
            pltpu.SemaphoreType.DMA((Q,)),
            pltpu.SemaphoreType.DMA((3, Q, N)),
            pltpu.SemaphoreType.DMA((Q, N)),
            pltpu.SemaphoreType.DMA((N,)),
            pltpu.SemaphoreType.DMA((N,)),
            pltpu.SemaphoreType.DMA((M,)),
            pltpu.SemaphoreType.DMA((M,)),
        ],
        compiler_params=pltpu.CompilerParams(collective_id=0, has_side_effects=True),
        name="legendre",
    )(coefficients, turned)

    lons = tendencies.shape[2]
    u, v, cb, sb = trig_tables(wavenumber, lons)
    tile = 512
    whole = lambda x: pl.BlockSpec(x.shape, lambda i: (0,) * x.ndim)
    grid_spec = pl.BlockSpec((tendencies.shape[0], tendencies.shape[1], tile), lambda i: (0, 0, i))
    perturbed = pl.pallas_call(
        functools.partial(synth_kernel, None),
        grid=(lons // tile,),
        out_shape=jax.ShapeDtypeStruct(tendencies.shape, jnp.bfloat16),
        in_specs=[whole(fourier), whole(u), whole(v), whole(cb), whole(sb), grid_spec],
        out_specs=grid_spec,
        scratch_shapes=[
            pltpu.VMEM((tendencies.shape[0] * tendencies.shape[1], u.shape[0]), jnp.bfloat16),
            pltpu.VMEM((u.shape[0], tile), jnp.bfloat16),
        ],
        name="synthesis",
    )(fourier, u, v, cb, sb, tendencies)
    return (perturbed, new_state)


def solution(mesh):
    return jax.shard_map(
        functools.partial(per_device, mesh.shape["mem"], mesh.shape["ma"]),
        mesh=mesh,
        in_specs=(
            P(None, "mem", "ma", None, None),
            P(None, "mem", "ma", None, None),
            P(),
            P(),
            P(),
            P("ma", None, "mem"),
            P("mem", "ma", None),
        ),
        out_specs=(P("mem", "ma", None), P(None, "mem", "ma", None, None)),
        check_vma=False,
    )
```

```python
import functools
import math

import jax
import jax.numpy as jnp
from jax import lax
from jax.experimental import pallas as pl
from jax.experimental.pallas import tpu as pltpu
from jax.sharding import PartitionSpec as P

clip_level = 0.9
MESH = pl.DeviceIdType.MESH
PACK = 4


def legendre_kernel(N, M, c_ref, t_hbm, u_ref, v_ref, cb_ref, sb_ref, o_ref, basis_hbm, basis, gath, tabs, prod, send, land,
                    bsem, tsem, lsem, ssem, rsem, s1, r1, s2, r2):
    Z = N // 2
    Q = c_ref.shape[0]
    L = tabs.shape[1] // PACK
    R = N // M
    me = lax.axis_index("mem")
    mk = lax.axis_index("ma")
    z, p = lax.div(me, 2), lax.rem(me, 2)
    mate = z * 2 + 1 - p

    barrier = pltpu.get_barrier_semaphore()
    for d in range(1, N):
        pl.semaphore_signal(barrier, inc=1, device_id={"mem": lax.rem(me + d, N)}, device_id_type=MESH)
    for d in range(1, M):
        pl.semaphore_signal(barrier, inc=1, device_id={"ma": lax.rem(mk + d, M)}, device_id_type=MESH)

    def table_copy(q):
        return pltpu.make_async_copy(t_hbm.at[q], tabs.at[q], tsem.at[q])

    def own_copy(q):
        return pltpu.make_async_copy(c_ref.at[q], gath.at[q, me], lsem.at[q])

    def hop(way, q, src, ref, dst):
        return pltpu.make_async_remote_copy(
            src_ref=ref, dst_ref=gath.at[q, src], send_sem=ssem.at[way, q, src],
            recv_sem=rsem.at[q, src], device_id={"mem": dst}, device_id_type=MESH)

    pl.semaphore_wait(barrier, N - 1 + M - 1)

    @pl.loop(0, Q)
    def _(q):
        @pl.when(z + 1 < Z)
        def _():
            hop(0, q, me, c_ref.at[q], me + 2).start()

        @pl.when(z > 0)
        def _():
            hop(1, q, me, c_ref.at[q], me - 2).start()

        hop(2, q, me, c_ref.at[q], mate).start()
        own_copy(q).start()
        table_copy(q).start()

    def arrived(q, src):
        hop(2, q, src, gath.at[q, src], mate).wait_recv()

    def relay(q, src, way, more, dst):
        arrived(q, src)

        @pl.when(more)
        def _():
            hop(way, q, src, gath.at[q, src], dst).start()

        hop(2, q, src, gath.at[q, src], mate).start()

    steps = Q + Z - 2
    cols = basis.shape[2] // 128

    def basis_copy(s):
        return pltpu.make_async_copy(
            basis.at[s], basis_hbm.at[:, pl.ds(s * cols * 128, cols * 128)], bsem.at[s])

    @pl.loop(0, steps)
    def _(s):
        width = u_ref.shape[1]
        turn = lax.rem(width - s * cols, width)
        u = pltpu.roll(u_ref[...], turn, 1)
        v = pltpu.roll(v_ref[...], turn, 1)
        for a in range(cols):
            value = u[:, a:a + 1] * cb_ref[...] + v[:, a:a + 1] * sb_ref[...]
            basis[s, :, a * 128:(a + 1) * 128] = value.astype(jnp.bfloat16)
        basis_copy(s).start()
        for h in range(1, Z):
            q = s - h + 1
            live = jnp.logical_and(q >= 0, q < Q)

            @pl.when(jnp.logical_and(live, z - h >= 0))
            def _():
                relay(q, me - 2 * h, 0, z + 1 < Z, me + 2)

            @pl.when(jnp.logical_and(live, z + h < Z))
            def _():
                relay(q, me + 2 * h, 1, z > 0, me - 2)

        q = s - (Z - 2)

        @pl.when(q >= 0)
        def _():
            own_copy(q).wait()
            table_copy(q).wait()
            for i in range(Z):
                arrived(q, 2 * i + 1 - p)
            lhs = gath[q].reshape(-1, gath.shape[3])
            full = lax.dot_general(lhs, tabs[q], (((1,), (1,)), ((), ())), preferred_element_type=jnp.float32)
            slot = lax.broadcasted_iota(jnp.int32, (full.shape[0], L), 0) // 2 % PACK
            diag = full[:, :L]
            for j in range(1, PACK):
                diag = jnp.where(slot == j, full[:, j * L:(j + 1) * L], diag)
            prod[:, :, q] = diag.reshape(prod.shape[0], prod.shape[1], 2 * PACK, L)

    H = send.shape[1]

    def out1(dst):
        return pltpu.make_async_remote_copy(
            src_ref=send.at[dst], dst_ref=land.at[me], send_sem=s1.at[dst],
            recv_sem=r1.at[me], device_id={"mem": dst}, device_id_type=MESH)

    def in1(src):
        return pltpu.make_async_remote_copy(
            src_ref=send.at[src], dst_ref=land.at[src], send_sem=s1.at[src],
            recv_sem=r1.at[src], device_id={"mem": src}, device_id_type=MESH)

    @pl.loop(1, N)
    def _(d):
        dst = lax.rem(me + d, N)
        for h in range(H):
            block = prod[dst * H + h].reshape(-1, L)
            send[dst, h] = block.T.astype(jnp.bfloat16)
        out1(dst).start()

    for h in range(H):
        block = prod[me * H + h].reshape(-1, L)
        land[me, h] = block.T.astype(jnp.bfloat16)

    def out2(kk):
        return pltpu.make_async_remote_copy(
            src_ref=land.at[pl.ds(R * kk, R)], dst_ref=o_ref.at[mk], send_sem=s2.at[kk],
            recv_sem=r2.at[mk], device_id={"ma": kk}, device_id_type=MESH)

    def in2(kk):
        return pltpu.make_async_remote_copy(
            src_ref=land.at[pl.ds(R * kk, R)], dst_ref=o_ref.at[kk], send_sem=s2.at[kk],
            recv_sem=r2.at[kk], device_id={"ma": kk}, device_id_type=MESH)

    def gather_rows(kk):
        for r in range(R):
            src = R * kk + r

            @pl.when(src != me)
            def _():
                in1(src).wait_recv()

    for d in range(1, M):
        kk = lax.rem(mk + d, M)
        gather_rows(kk)
        out2(kk).start()
    gather_rows(mk)
    o_ref[mk] = land[pl.ds(R * mk, R)]
    for d in range(1, M):
        in2(lax.rem(mk + d, M)).wait_recv()

    @pl.loop(0, steps)
    def _(s):
        basis_copy(s).wait()

    for d in range(1, M):
        out2(lax.rem(mk + d, M)).wait_send()

    @pl.loop(1, N)
    def _(d):
        out1(lax.rem(me + d, N)).wait_send()

    @pl.loop(0, Q)
    def _(q):
        for i in range(Z):
            src = 2 * i + p
            ref = gath.at[q, src]

            @pl.when(jnp.logical_and(z + 1 < Z, z >= i))
            def _():
                hop(0, q, src, ref, me + 2).wait_send()

            @pl.when(jnp.logical_and(z > 0, z <= i))
            def _():
                hop(1, q, src, ref, me - 2).wait_send()

            hop(2, q, src, ref, mate).wait_send()


def update_kernel(m_ref, d_ref, amp_ref, s_ref, f_ref, n_ref, c_ref, u_ref, v_ref, cb_ref, sb_ref, total, lons):
    step = pl.program_id(0)
    scales, members, _, _, degrees = s_ref.shape
    first = lax.axis_index("ma") * (pl.num_programs(0) * PACK) + step * PACK
    degree = lax.broadcasted_iota(jnp.int32, (2, degrees), 1)
    for j in range(PACK):
        kept = jnp.where(degree >= m_ref[first + j], 1.0, 0.0).astype(jnp.float32)
        for b in range(members):
            acc = None
            for i in range(scales):
                new = kept * (d_ref[i] * s_ref[i, b, j] + amp_ref[i:i + 1, :] * f_ref[i, b, j])
                n_ref[i, b, j] = new
                acc = new if acc is None else acc + new
            total[b * 2 * PACK + 2 * j:b * 2 * PACK + 2 * j + 2, :] = acc
    c_ref[0] = total[...].astype(jnp.bfloat16)

    unit = 2.0 * math.pi / lons
    width = u_ref.shape[1]
    group = lax.broadcasted_iota(jnp.int32, (8, 1), 0)
    shift = (group % 2).astype(jnp.float32) * (lons // 4)

    def angle(x):
        return (x - lons * jnp.floor(x * (1.0 / lons))) * unit

    for g in range(u_ref.shape[0] // 8):
        at = (step * (u_ref.shape[0] // 8) + g) * PACK
        m = m_ref[at]
        near = jnp.full((8, 128), m, jnp.int32)
        far = jnp.full((8, width), lax.rem(m * 128, lons), jnp.int32)
        for j in range(1, PACK):
            m = m_ref[at + j]
            near = jnp.where(group // 2 == j, m, near)
            far = jnp.where(group // 2 == j, lax.rem(m * 128, lons), far)
        near = near * lax.broadcasted_iota(jnp.int32, (8, 128), 1)
        far = far * lax.broadcasted_iota(jnp.int32, (8, width), 1)
        near = angle(near.astype(jnp.float32))
        far = angle(far.astype(jnp.float32) + shift)
        u_ref[g * 8:(g + 1) * 8] = jnp.cos(far)
        v_ref[g * 8:(g + 1) * 8] = -jnp.sin(far)
        cb_ref[g * 8:(g + 1) * 8] = jnp.cos(near)
        sb_ref[g * 8:(g + 1) * 8] = jnp.sin(near)


def synth_kernel(f_ref, basis_ref, t_ref, o_ref, lhs):
    M, R, H, L, W = f_ref.shape
    half = W // 2

    @pl.when(pl.program_id(0) == 0)
    def _():
        parts = []
        for b in range(2 * H):
            for r in range(R):
                lo = (b % 2) * half
                row = [f_ref[k, r, b // 2].astype(jnp.float32)[:, lo:lo + half] for k in range(M)]
                parts.append(jnp.concatenate(row, axis=1))
        lhs[...] = jnp.concatenate(parts, axis=0).astype(jnp.bfloat16)

    pattern = jnp.dot(lhs[...], basis_ref[...], preferred_element_type=jnp.float32)
    scale = 1.0 / math.sqrt(basis_ref.shape[0] // 2)
    factor = jnp.clip(pattern * scale + 1.0, 1.0 - clip_level, 1.0 + clip_level)
    o_ref[...] = (t_ref[...].astype(jnp.float32) * factor.reshape(o_ref.shape)).astype(jnp.bfloat16)


def per_device(N, M, ar_state, forcing, ar_decay, amplitude, wavenumber, tables, tendencies):
    members, waves = ar_state.shape[1], ar_state.shape[2]
    degrees = ar_state.shape[4]
    lats = tables.shape[2]
    Q = waves // PACK
    rows = members * 2 * PACK
    scales = ar_state.shape[0]
    lons = tendencies.shape[2]
    modes = 2 * wavenumber.shape[0]
    width = -(-(lons // 128) // 128) * 128
    state_spec = pl.BlockSpec((scales, members, PACK, 2, degrees), lambda i: (0, 0, i, 0, 0))
    smem = pl.BlockSpec(memory_space=pltpu.SMEM)
    trig = lambda w: (pl.BlockSpec((modes // Q, w), lambda i: (i, 0)), jax.ShapeDtypeStruct((modes, w), jnp.float32))
    tables_out = [trig(width), trig(width), trig(128), trig(128)]
    new_state, coefficients, u, v, cb, sb = pl.pallas_call(
        functools.partial(update_kernel, lons=lons),
        grid=(Q,),
        out_shape=[
            jax.ShapeDtypeStruct(ar_state.shape, jnp.float32),
            jax.ShapeDtypeStruct((Q, rows, degrees), jnp.bfloat16),
        ] + [x[1] for x in tables_out],
        in_specs=[smem, smem, pl.BlockSpec(amplitude.shape, lambda i: (0, 0)), state_spec, state_spec],
        out_specs=[state_spec, pl.BlockSpec((1, rows, degrees), lambda i: (i, 0, 0))] + [x[0] for x in tables_out],
        scratch_shapes=[
            pltpu.VMEM((rows, degrees), jnp.float32),
        ],
        name="update",
    )(wavenumber, ar_decay, amplitude, ar_state, forcing)
    turned = tables.transpose(0, 2, 1).reshape(Q, PACK * lats, degrees)

    H = members // 2
    W = 2 * Q * 2 * PACK
    R = N // M
    any_spec = pl.BlockSpec(memory_space=pl.ANY)
    vmem_spec = pl.BlockSpec(memory_space=pltpu.VMEM)
    steps = Q + N // 2 - 2
    cols = lons // 128 // steps
    fourier, basis = pl.pallas_call(
        functools.partial(legendre_kernel, N, M),
        out_shape=[
            jax.ShapeDtypeStruct((M, R, H, lats, W), jnp.bfloat16),
            jax.ShapeDtypeStruct((modes, lons), jnp.bfloat16),
        ],
        in_specs=[vmem_spec, any_spec] + [vmem_spec] * 4,
        out_specs=[vmem_spec, any_spec],
        scratch_shapes=[
            pltpu.VMEM((steps, modes, cols * 128), jnp.bfloat16),
            pltpu.VMEM((Q, N, rows, degrees), jnp.bfloat16),
            pltpu.VMEM((Q, PACK * lats, degrees), jnp.bfloat16),
            pltpu.VMEM((N * H, 2, Q, 2 * PACK, lats), jnp.float32),
            pltpu.VMEM((N, H, lats, W), jnp.bfloat16),
            pltpu.VMEM((N, H, lats, W), jnp.bfloat16),
            pltpu.SemaphoreType.DMA((steps,)),
            pltpu.SemaphoreType.DMA((Q,)),
            pltpu.SemaphoreType.DMA((Q,)),
            pltpu.SemaphoreType.DMA((3, Q, N)),
            pltpu.SemaphoreType.DMA((Q, N)),
            pltpu.SemaphoreType.DMA((N,)),
            pltpu.SemaphoreType.DMA((N,)),
            pltpu.SemaphoreType.DMA((M,)),
            pltpu.SemaphoreType.DMA((M,)),
        ],
        compiler_params=pltpu.CompilerParams(collective_id=0, has_side_effects=True),
        name="legendre",
    )(coefficients, turned, u, v, cb, sb)

    tile = lons // 5
    grid_spec = pl.BlockSpec((tendencies.shape[0], tendencies.shape[1], tile), lambda i: (0, 0, i))
    perturbed = pl.pallas_call(
        synth_kernel,
        grid=(lons // tile,),
        out_shape=jax.ShapeDtypeStruct(tendencies.shape, jnp.bfloat16),
        in_specs=[
            pl.BlockSpec(fourier.shape, lambda i: (0,) * 5),
            pl.BlockSpec((modes, tile), lambda i: (0, i)),
            grid_spec,
        ],
        out_specs=grid_spec,
        scratch_shapes=[pltpu.VMEM((tendencies.shape[0] * tendencies.shape[1], modes), jnp.bfloat16)],
        name="synthesis",
    )(fourier, basis, tendencies)
    return (perturbed, new_state)


def solution(mesh):
    return jax.shard_map(
        functools.partial(per_device, mesh.shape["mem"], mesh.shape["ma"]),
        mesh=mesh,
        in_specs=(
            P(None, "mem", "ma", None, None),
            P(None, "mem", "ma", None, None),
            P(),
            P(),
            P(),
            P("ma", None, "mem"),
            P("mem", "ma", None),
        ),
        out_specs=(P("mem", "ma", None), P(None, "mem", "ma", None, None)),
        check_vma=False,
    )
```

```python
import functools
import math

import jax
import jax.numpy as jnp
from jax import lax
from jax.experimental import pallas as pl
from jax.experimental.pallas import tpu as pltpu
from jax.sharding import PartitionSpec as P

clip_level = 0.9
MESH = pl.DeviceIdType.MESH
PACK = 4


def tail_chunks(chunks, chips):
    return chunks // 4 if chips >= 4 else 0


def legendre_kernel(N, M, c_ref, t_hbm, u_ref, v_ref, cb_ref, sb_ref, o_ref, basis_hbm, basis, gath, tabs, prod, send, land,
                    adopt, prod2, send2, land2,
                    bsem, tsem, lsem, ssem, rsem, s1, r1, s2, r2, asend, arecv, s1b, r1b):
    Z = N // 2
    Q = c_ref.shape[0]
    L = tabs.shape[1] // PACK
    R = N // M
    me = lax.axis_index("mem")
    mk = lax.axis_index("ma")
    z, p = lax.div(me, 2), lax.rem(me, 2)
    mate = z * 2 + 1 - p
    E = tail_chunks(Q, Z)
    end = jnp.logical_or(z == 0, z == Z - 1)
    adopter = jnp.logical_or(z == 1, z == Z - 2)
    inner = jnp.where(z == 0, me + 2, me - 2)
    corner = p + jnp.where(z == Z - 2, 2, 0)

    def here(q):
        return jnp.logical_not(jnp.logical_and(end, q >= Q - E))

    def goes_up(q):
        return jnp.logical_and(z + 1 < Z, jnp.logical_not(jnp.logical_and(z == Z - 2, q >= Q - E)))

    def goes_down(q):
        return jnp.logical_and(z > 0, jnp.logical_not(jnp.logical_and(z == 1, q >= Q - E)))

    barrier = pltpu.get_barrier_semaphore()
    for d in range(1, N):
        pl.semaphore_signal(barrier, inc=1, device_id={"mem": lax.rem(me + d, N)}, device_id_type=MESH)
    for d in range(1, M):
        pl.semaphore_signal(barrier, inc=1, device_id={"ma": lax.rem(mk + d, M)}, device_id_type=MESH)

    def table_copy(q):
        return pltpu.make_async_copy(t_hbm.at[q], tabs.at[q], tsem.at[q])

    def own_copy(q):
        return pltpu.make_async_copy(c_ref.at[q], gath.at[q, me], lsem.at[q])

    def hop(way, q, src, ref, dst):
        return pltpu.make_async_remote_copy(
            src_ref=ref, dst_ref=gath.at[q, src], send_sem=ssem.at[way, q, src],
            recv_sem=rsem.at[q, src], device_id={"mem": dst}, device_id_type=MESH)

    pl.semaphore_wait(barrier, N - 1 + M - 1)

    @pl.loop(0, Q)
    def _(q):
        @pl.when(goes_up(q))
        def _():
            hop(0, q, me, c_ref.at[q], me + 2).start()

        @pl.when(goes_down(q))
        def _():
            hop(1, q, me, c_ref.at[q], me - 2).start()

        @pl.when(here(q))
        def _():
            hop(2, q, me, c_ref.at[q], mate).start()
            own_copy(q).start()

        table_copy(q).start()

    def adopt_copy(e):
        return pltpu.make_async_remote_copy(
            src_ref=tabs.at[Q - E + e], dst_ref=adopt.at[e], send_sem=asend.at[e],
            recv_sem=arecv.at[e], device_id={"mem": inner}, device_id_type=MESH)

    for e in range(E):
        @pl.when(end)
        def _():
            table_copy(Q - E + e).wait()
            adopt_copy(e).start()

    def arrived(q, src):
        hop(2, q, src, gath.at[q, src], mate).wait_recv()

    def relay(q, src, way, more, dst):
        arrived(q, src)

        @pl.when(more)
        def _():
            hop(way, q, src, gath.at[q, src], dst).start()

        hop(2, q, src, gath.at[q, src], mate).start()

    steps = Q + Z - 2
    cols = basis.shape[2] // 128

    def basis_copy(s):
        return pltpu.make_async_copy(
            basis.at[s], basis_hbm.at[:, pl.ds(s * cols * 128, cols * 128)], bsem.at[s])

    @pl.loop(0, steps)
    def _(s):
        width = u_ref.shape[1]
        turn = lax.rem(width - s * cols, width)
        u = pltpu.roll(u_ref[...], turn, 1)
        v = pltpu.roll(v_ref[...], turn, 1)
        for a in range(cols):
            value = u[:, a:a + 1] * cb_ref[...] + v[:, a:a + 1] * sb_ref[...]
            basis[s, :, a * 128:(a + 1) * 128] = value.astype(jnp.bfloat16)
        basis_copy(s).start()
        for h in range(1, Z):
            q = s - h + 1
            live = jnp.logical_and(q >= 0, q < Q)

            live = jnp.logical_and(live, here(q))

            @pl.when(jnp.logical_and(live, z - h >= 0))
            def _():
                relay(q, me - 2 * h, 0, goes_up(q), me + 2)

            @pl.when(jnp.logical_and(live, z + h < Z))
            def _():
                relay(q, me + 2 * h, 1, goes_down(q), me - 2)

        q = s - (Z - 2)

        def rows_of(table):
            lhs = gath[q].reshape(-1, gath.shape[3])
            full = lax.dot_general(lhs, table, (((1,), (1,)), ((), ())), preferred_element_type=jnp.float32)
            slot = lax.broadcasted_iota(jnp.int32, (full.shape[0], L), 0) // 2 % PACK
            diag = full[:, :L]
            for j in range(1, PACK):
                diag = jnp.where(slot == j, full[:, j * L:(j + 1) * L], diag)
            return diag.reshape(prod.shape[0], prod.shape[1], 2 * PACK, L)

        @pl.when(jnp.logical_and(q >= 0, here(q)))
        def _():
            own_copy(q).wait()
            table_copy(q).wait()
            for i in range(Z):
                arrived(q, 2 * i + 1 - p)
            prod[:, :, q] = rows_of(tabs[q])

        if E:
            @pl.when(jnp.logical_not(here(q)))
            def _():
                prod[:, :, q] = jnp.zeros((prod.shape[0], prod.shape[1], 2 * PACK, L), jnp.float32)

            @pl.when(jnp.logical_and(adopter, q >= Q - E))
            def _():
                e = q - (Q - E)
                adopt_copy(e).wait_recv()
                prod2[:, :, e] = rows_of(adopt[e])

    H = send.shape[1]

    def out1(dst):
        return pltpu.make_async_remote_copy(
            src_ref=send.at[dst], dst_ref=land.at[me], send_sem=s1.at[dst],
            recv_sem=r1.at[me], device_id={"mem": dst}, device_id_type=MESH)

    def in1(src):
        return pltpu.make_async_remote_copy(
            src_ref=send.at[src], dst_ref=land.at[src], send_sem=s1.at[src],
            recv_sem=r1.at[src], device_id={"mem": src}, device_id_type=MESH)

    @pl.loop(1, N)
    def _(d):
        dst = lax.rem(me + d, N)
        for h in range(H):
            block = prod[dst * H + h].reshape(-1, L)
            send[dst, h] = block.T.astype(jnp.bfloat16)
        out1(dst).start()

    for h in range(H):
        block = prod[me * H + h].reshape(-1, L)
        land[me, h] = block.T.astype(jnp.bfloat16)

    def out1b(dst):
        return pltpu.make_async_remote_copy(
            src_ref=send2.at[dst], dst_ref=land2.at[corner], send_sem=s1b.at[dst],
            recv_sem=r1b.at[corner], device_id={"mem": dst}, device_id_type=MESH)

    def in1b(e, src):
        return pltpu.make_async_remote_copy(
            src_ref=send2.at[src], dst_ref=land2.at[e], send_sem=s1b.at[src],
            recv_sem=r1b.at[e], device_id={"mem": src}, device_id_type=MESH)

    def spare_rows(dst, h):
        at = dst * H + h
        block = jnp.concatenate([prod[at][:, :Q - E], prod2[at]], axis=1).reshape(-1, L)
        return block.T.astype(jnp.bfloat16)

    if E:
        @pl.when(adopter)
        def _():
            @pl.loop(1, N)
            def _(d):
                dst = lax.rem(me + d, N)
                for h in range(H):
                    send2[dst, h] = spare_rows(dst, h)
                out1b(dst).start()

            for h in range(H):
                land2[corner, h] = spare_rows(me, h)

    def out2(kk):
        return pltpu.make_async_remote_copy(
            src_ref=land.at[pl.ds(R * kk, R)], dst_ref=o_ref.at[mk], send_sem=s2.at[kk],
            recv_sem=r2.at[mk], device_id={"ma": kk}, device_id_type=MESH)

    def in2(kk):
        return pltpu.make_async_remote_copy(
            src_ref=land.at[pl.ds(R * kk, R)], dst_ref=o_ref.at[kk], send_sem=s2.at[kk],
            recv_sem=r2.at[kk], device_id={"ma": kk}, device_id_type=MESH)

    def gather_rows(kk):
        for r in range(R):
            src = R * kk + r

            @pl.when(src != me)
            def _():
                in1(src).wait_recv()

            if E:
                low, high = src < 2, src >= N - 2
                helper = jnp.where(low, src + 2, src - 2)
                e = lax.rem(src, 2) + jnp.where(high, 2, 0)

                @pl.when(jnp.logical_and(jnp.logical_or(low, high), helper != me))
                def _():
                    in1b(e, helper).wait_recv()

                @pl.when(jnp.logical_or(low, high))
                def _():
                    lane = lax.broadcasted_iota(jnp.int32, land.shape[2:], 1)
                    spare = lane % (2 * PACK * Q) >= 2 * PACK * (Q - E)
                    for h in range(H):
                        own = land[src, h].astype(jnp.float32)
                        other = land2[e, h].astype(jnp.float32)
                        land[src, h] = jnp.where(spare, other, own).astype(jnp.bfloat16)

    for d in range(1, M):
        kk = lax.rem(mk + d, M)
        gather_rows(kk)
        out2(kk).start()
    gather_rows(mk)
    o_ref[mk] = land[pl.ds(R * mk, R)]
    for d in range(1, M):
        in2(lax.rem(mk + d, M)).wait_recv()

    @pl.loop(0, steps)
    def _(s):
        basis_copy(s).wait()

    for d in range(1, M):
        out2(lax.rem(mk + d, M)).wait_send()

    @pl.loop(1, N)
    def _(d):
        out1(lax.rem(me + d, N)).wait_send()

    @pl.loop(0, Q)
    def _(q):
        for i in range(Z):
            src = 2 * i + p
            ref = gath.at[q, src]

            @pl.when(jnp.logical_and(goes_up(q), z >= i))
            def _():
                hop(0, q, src, ref, me + 2).wait_send()

            @pl.when(jnp.logical_and(goes_down(q), z <= i))
            def _():
                hop(1, q, src, ref, me - 2).wait_send()

            @pl.when(here(q))
            def _():
                hop(2, q, src, ref, mate).wait_send()

    if E:
        @pl.when(end)
        def _():
            for e in range(E):
                adopt_copy(e).wait_send()

        @pl.when(adopter)
        def _():
            @pl.loop(1, N)
            def _(d):
                out1b(lax.rem(me + d, N)).wait_send()


def update_kernel(m_ref, d_ref, amp_ref, s_ref, f_ref, n_ref, c_ref, u_ref, v_ref, cb_ref, sb_ref, total, lons):
    step = pl.program_id(0)
    scales, members, _, _, degrees = s_ref.shape
    first = lax.axis_index("ma") * (pl.num_programs(0) * PACK) + step * PACK
    degree = lax.broadcasted_iota(jnp.int32, (2, degrees), 1)
    for j in range(PACK):
        kept = jnp.where(degree >= m_ref[first + j], 1.0, 0.0).astype(jnp.float32)
        for b in range(members):
            acc = None
            for i in range(scales):
                new = kept * (d_ref[i] * s_ref[i, b, j] + amp_ref[i:i + 1, :] * f_ref[i, b, j])
                n_ref[i, b, j] = new
                acc = new if acc is None else acc + new
            total[b * 2 * PACK + 2 * j:b * 2 * PACK + 2 * j + 2, :] = acc
    c_ref[0] = total[...].astype(jnp.bfloat16)

    unit = 2.0 * math.pi / lons
    width = u_ref.shape[1]
    group = lax.broadcasted_iota(jnp.int32, (8, 1), 0)
    shift = (group % 2).astype(jnp.float32) * (lons // 4)

    def angle(x):
        return (x - lons * jnp.floor(x * (1.0 / lons))) * unit

    for g in range(u_ref.shape[0] // 8):
        at = (step * (u_ref.shape[0] // 8) + g) * PACK
        m = m_ref[at]
        near = jnp.full((8, 128), m, jnp.int32)
        far = jnp.full((8, width), lax.rem(m * 128, lons), jnp.int32)
        for j in range(1, PACK):
            m = m_ref[at + j]
            near = jnp.where(group // 2 == j, m, near)
            far = jnp.where(group // 2 == j, lax.rem(m * 128, lons), far)
        near = near * lax.broadcasted_iota(jnp.int32, (8, 128), 1)
        far = far * lax.broadcasted_iota(jnp.int32, (8, width), 1)
        near = angle(near.astype(jnp.float32))
        far = angle(far.astype(jnp.float32) + shift)
        u_ref[g * 8:(g + 1) * 8] = jnp.cos(far)
        v_ref[g * 8:(g + 1) * 8] = -jnp.sin(far)
        cb_ref[g * 8:(g + 1) * 8] = jnp.cos(near)
        sb_ref[g * 8:(g + 1) * 8] = jnp.sin(near)


def synth_kernel(f_ref, basis_ref, t_ref, o_ref, lhs):
    M, R, H, L, W = f_ref.shape
    half = W // 2

    @pl.when(pl.program_id(0) == 0)
    def _():
        parts = []
        for b in range(2 * H):
            for r in range(R):
                lo = (b % 2) * half
                row = [f_ref[k, r, b // 2].astype(jnp.float32)[:, lo:lo + half] for k in range(M)]
                parts.append(jnp.concatenate(row, axis=1))
        lhs[...] = jnp.concatenate(parts, axis=0).astype(jnp.bfloat16)

    pattern = jnp.dot(lhs[...], basis_ref[...], preferred_element_type=jnp.float32)
    scale = 1.0 / math.sqrt(basis_ref.shape[0] // 2)
    factor = jnp.clip(pattern * scale + 1.0, 1.0 - clip_level, 1.0 + clip_level)
    o_ref[...] = (t_ref[...].astype(jnp.float32) * factor.reshape(o_ref.shape)).astype(jnp.bfloat16)


def per_device(N, M, ar_state, forcing, ar_decay, amplitude, wavenumber, tables, tendencies):
    members, waves = ar_state.shape[1], ar_state.shape[2]
    degrees = ar_state.shape[4]
    lats = tables.shape[2]
    Q = waves // PACK
    rows = members * 2 * PACK
    scales = ar_state.shape[0]
    lons = tendencies.shape[2]
    modes = 2 * wavenumber.shape[0]
    width = -(-(lons // 128) // 128) * 128
    state_spec = pl.BlockSpec((scales, members, PACK, 2, degrees), lambda i: (0, 0, i, 0, 0))
    smem = pl.BlockSpec(memory_space=pltpu.SMEM)
    trig = lambda w: (pl.BlockSpec((modes // Q, w), lambda i: (i, 0)), jax.ShapeDtypeStruct((modes, w), jnp.float32))
    tables_out = [trig(width), trig(width), trig(128), trig(128)]
    new_state, coefficients, u, v, cb, sb = pl.pallas_call(
        functools.partial(update_kernel, lons=lons),
        grid=(Q,),
        out_shape=[
            jax.ShapeDtypeStruct(ar_state.shape, jnp.float32),
            jax.ShapeDtypeStruct((Q, rows, degrees), jnp.bfloat16),
        ] + [x[1] for x in tables_out],
        in_specs=[smem, smem, pl.BlockSpec(amplitude.shape, lambda i: (0, 0)), state_spec, state_spec],
        out_specs=[state_spec, pl.BlockSpec((1, rows, degrees), lambda i: (i, 0, 0))] + [x[0] for x in tables_out],
        scratch_shapes=[
            pltpu.VMEM((rows, degrees), jnp.float32),
        ],
        name="update",
    )(wavenumber, ar_decay, amplitude, ar_state, forcing)
    turned = tables.transpose(0, 2, 1).reshape(Q, PACK * lats, degrees)

    H = members // 2
    W = 2 * Q * 2 * PACK
    R = N // M
    any_spec = pl.BlockSpec(memory_space=pl.ANY)
    vmem_spec = pl.BlockSpec(memory_space=pltpu.VMEM)
    steps = Q + N // 2 - 2
    spare = max(tail_chunks(Q, N // 2), 1)
    cols = lons // 128 // steps
    fourier, basis = pl.pallas_call(
        functools.partial(legendre_kernel, N, M),
        out_shape=[
            jax.ShapeDtypeStruct((M, R, H, lats, W), jnp.bfloat16),
            jax.ShapeDtypeStruct((modes, lons), jnp.bfloat16),
        ],
        in_specs=[vmem_spec, any_spec] + [vmem_spec] * 4,
        out_specs=[vmem_spec, any_spec],
        scratch_shapes=[
            pltpu.VMEM((steps, modes, cols * 128), jnp.bfloat16),
            pltpu.VMEM((Q, N, rows, degrees), jnp.bfloat16),
            pltpu.VMEM((Q, PACK * lats, degrees), jnp.bfloat16),
            pltpu.VMEM((N * H, 2, Q, 2 * PACK, lats), jnp.float32),
            pltpu.VMEM((N, H, lats, W), jnp.bfloat16),
            pltpu.VMEM((N, H, lats, W), jnp.bfloat16),
            pltpu.VMEM((spare, PACK * lats, degrees), jnp.bfloat16),
            pltpu.VMEM((N * H, 2, spare, 2 * PACK, lats), jnp.float32),
            pltpu.VMEM((N, H, lats, W), jnp.bfloat16),
            pltpu.VMEM((4, H, lats, W), jnp.bfloat16),
            pltpu.SemaphoreType.DMA((steps,)),
            pltpu.SemaphoreType.DMA((Q,)),
            pltpu.SemaphoreType.DMA((Q,)),
            pltpu.SemaphoreType.DMA((3, Q, N)),
            pltpu.SemaphoreType.DMA((Q, N)),
            pltpu.SemaphoreType.DMA((N,)),
            pltpu.SemaphoreType.DMA((N,)),
            pltpu.SemaphoreType.DMA((M,)),
            pltpu.SemaphoreType.DMA((M,)),
            pltpu.SemaphoreType.DMA((spare,)),
            pltpu.SemaphoreType.DMA((spare,)),
            pltpu.SemaphoreType.DMA((N,)),
            pltpu.SemaphoreType.DMA((4,)),
        ],
        compiler_params=pltpu.CompilerParams(collective_id=0, has_side_effects=True),
        name="legendre",
    )(coefficients, turned, u, v, cb, sb)

    tile = lons // 5
    grid_spec = pl.BlockSpec((tendencies.shape[0], tendencies.shape[1], tile), lambda i: (0, 0, i))
    perturbed = pl.pallas_call(
        synth_kernel,
        grid=(lons // tile,),
        out_shape=jax.ShapeDtypeStruct(tendencies.shape, jnp.bfloat16),
        in_specs=[
            pl.BlockSpec(fourier.shape, lambda i: (0,) * 5),
            pl.BlockSpec((modes, tile), lambda i: (0, i)),
            grid_spec,
        ],
        out_specs=grid_spec,
        scratch_shapes=[pltpu.VMEM((tendencies.shape[0] * tendencies.shape[1], modes), jnp.bfloat16)],
        name="synthesis",
    )(fourier, basis, tendencies)
    return (perturbed, new_state)


def solution(mesh):
    return jax.shard_map(
        functools.partial(per_device, mesh.shape["mem"], mesh.shape["ma"]),
        mesh=mesh,
        in_specs=(
            P(None, "mem", "ma", None, None),
            P(None, "mem", "ma", None, None),
            P(),
            P(),
            P(),
            P("ma", None, "mem"),
            P("mem", "ma", None),
        ),
        out_specs=(P("mem", "ma", None), P(None, "mem", "ma", None, None)),
        check_vma=False,
    )
```

```python
import functools
import math

import jax
import jax.numpy as jnp
from jax import lax
from jax.experimental import pallas as pl
from jax.experimental.pallas import tpu as pltpu
from jax.sharding import PartitionSpec as P

clip_level = 0.9
MESH = pl.DeviceIdType.MESH
PACK = 4
AHEAD = 2


def tail_chunks(chunks, chips):
    return chunks // 4 if chips >= 4 else 0


def legendre_kernel(N, M, c_ref, t_hbm, u_ref, v_ref, cb_ref, sb_ref, o_ref, basis_hbm, basis, gath, tabs, prod, send, land,
                    adopt, prod2, send2, land2,
                    bsem, tsem, lsem, ssem, rsem, s1, r1, s2, r2, asend, arecv, s1b, r1b):
    Z = N // 2
    Q = c_ref.shape[0]
    L = tabs.shape[1] // PACK
    R = N // M
    me = lax.axis_index("mem")
    mk = lax.axis_index("ma")
    z, p = lax.div(me, 2), lax.rem(me, 2)
    mate = z * 2 + 1 - p
    E = tail_chunks(Q, Z)
    end = jnp.logical_or(z == 0, z == Z - 1)
    adopter = jnp.logical_or(z == 1, z == Z - 2)
    inner = jnp.where(z == 0, me + 2, me - 2)
    corner = p + jnp.where(z == Z - 2, 2, 0)

    def here(q):
        return jnp.logical_not(jnp.logical_and(end, q >= Q - E))

    def goes_up(q):
        return jnp.logical_and(z + 1 < Z, jnp.logical_not(jnp.logical_and(z == Z - 2, q >= Q - E)))

    def goes_down(q):
        return jnp.logical_and(z > 0, jnp.logical_not(jnp.logical_and(z == 1, q >= Q - E)))

    barrier = pltpu.get_barrier_semaphore()
    for d in range(1, N):
        pl.semaphore_signal(barrier, inc=1, device_id={"mem": lax.rem(me + d, N)}, device_id_type=MESH)
    for d in range(1, M):
        pl.semaphore_signal(barrier, inc=1, device_id={"ma": lax.rem(mk + d, M)}, device_id_type=MESH)

    def table_copy(q):
        return pltpu.make_async_copy(t_hbm.at[q], tabs.at[q], tsem.at[q])

    def own_copy(q):
        return pltpu.make_async_copy(c_ref.at[q], gath.at[q, me], lsem.at[q])

    def hop(way, q, src, ref, dst):
        return pltpu.make_async_remote_copy(
            src_ref=ref, dst_ref=gath.at[q, src], send_sem=ssem.at[way, q, src],
            recv_sem=rsem.at[q, src], device_id={"mem": dst}, device_id_type=MESH)

    def send_own(q):
        @pl.when(goes_up(q))
        def _():
            hop(0, q, me, c_ref.at[q], me + 2).start()

        @pl.when(goes_down(q))
        def _():
            hop(1, q, me, c_ref.at[q], me - 2).start()

    pl.semaphore_wait(barrier, N - 1 + M - 1)

    @pl.loop(0, Q)
    def _(q):
        @pl.when(jnp.logical_or(end, q < AHEAD))
        def _():
            send_own(q)

        @pl.when(here(q))
        def _():
            hop(2, q, me, c_ref.at[q], mate).start()
            own_copy(q).start()

        table_copy(q).start()

    def adopt_copy(e):
        return pltpu.make_async_remote_copy(
            src_ref=tabs.at[Q - E + e], dst_ref=adopt.at[e], send_sem=asend.at[e],
            recv_sem=arecv.at[e], device_id={"mem": inner}, device_id_type=MESH)

    for e in range(E):
        @pl.when(end)
        def _():
            table_copy(Q - E + e).wait()
            adopt_copy(e).start()

    def arrived(q, src):
        hop(2, q, src, gath.at[q, src], mate).wait_recv()

    def relay(q, src, way, more, dst):
        arrived(q, src)

        @pl.when(more)
        def _():
            hop(way, q, src, gath.at[q, src], dst).start()

        hop(2, q, src, gath.at[q, src], mate).start()

    steps = Q + Z - 2
    cols = basis.shape[2] // 128

    def basis_copy(s):
        return pltpu.make_async_copy(
            basis.at[s], basis_hbm.at[:, pl.ds(s * cols * 128, cols * 128)], bsem.at[s])

    @pl.loop(0, steps)
    def _(s):
        @pl.when(jnp.logical_and(jnp.logical_not(end), s + AHEAD < Q))
        def _():
            send_own(s + AHEAD)

        width = u_ref.shape[1]
        turn = lax.rem(width - s * cols, width)
        u = pltpu.roll(u_ref[...], turn, 1)
        v = pltpu.roll(v_ref[...], turn, 1)
        for a in range(cols):
            value = u[:, a:a + 1] * cb_ref[...] + v[:, a:a + 1] * sb_ref[...]
            basis[s, :, a * 128:(a + 1) * 128] = value.astype(jnp.bfloat16)
        basis_copy(s).start()
        for h in range(1, Z):
            q = s - h + 1
            live = jnp.logical_and(q >= 0, q < Q)

            live = jnp.logical_and(live, here(q))

            @pl.when(jnp.logical_and(live, z - h >= 0))
            def _():
                relay(q, me - 2 * h, 0, goes_up(q), me + 2)

            @pl.when(jnp.logical_and(live, z + h < Z))
            def _():
                relay(q, me + 2 * h, 1, goes_down(q), me - 2)

        q = s - (Z - 2)

        def rows_of(table):
            lhs = gath[q].reshape(-1, gath.shape[3])
            full = lax.dot_general(lhs, table, (((1,), (1,)), ((), ())), preferred_element_type=jnp.float32)
            slot = lax.broadcasted_iota(jnp.int32, (full.shape[0], L), 0) // 2 % PACK
            diag = full[:, :L]
            for j in range(1, PACK):
                diag = jnp.where(slot == j, full[:, j * L:(j + 1) * L], diag)
            return diag.reshape(prod.shape[0], prod.shape[1], 2 * PACK, L)

        @pl.when(jnp.logical_and(q >= 0, here(q)))
        def _():
            own_copy(q).wait()
            table_copy(q).wait()
            for i in range(Z):
                arrived(q, 2 * i + 1 - p)
            prod[:, :, q] = rows_of(tabs[q])

        if E:
            @pl.when(jnp.logical_not(here(q)))
            def _():
                prod[:, :, q] = jnp.zeros((prod.shape[0], prod.shape[1], 2 * PACK, L), jnp.float32)

            @pl.when(jnp.logical_and(adopter, q >= Q - E))
            def _():
                e = q - (Q - E)
                adopt_copy(e).wait_recv()
                prod2[:, :, e] = rows_of(adopt[e])

    H = send.shape[1]

    def out1(dst):
        return pltpu.make_async_remote_copy(
            src_ref=send.at[dst], dst_ref=land.at[me], send_sem=s1.at[dst],
            recv_sem=r1.at[me], device_id={"mem": dst}, device_id_type=MESH)

    def in1(src):
        return pltpu.make_async_remote_copy(
            src_ref=send.at[src], dst_ref=land.at[src], send_sem=s1.at[src],
            recv_sem=r1.at[src], device_id={"mem": src}, device_id_type=MESH)

    @pl.loop(1, N)
    def _(d):
        dst = lax.rem(me + d, N)
        for h in range(H):
            block = prod[dst * H + h].reshape(-1, L)
            send[dst, h] = block.T.astype(jnp.bfloat16)
        out1(dst).start()

    for h in range(H):
        block = prod[me * H + h].reshape(-1, L)
        land[me, h] = block.T.astype(jnp.bfloat16)

    def out1b(dst):
        return pltpu.make_async_remote_copy(
            src_ref=send2.at[dst], dst_ref=land2.at[corner], send_sem=s1b.at[dst],
            recv_sem=r1b.at[corner], device_id={"mem": dst}, device_id_type=MESH)

    def in1b(e, src):
        return pltpu.make_async_remote_copy(
            src_ref=send2.at[src], dst_ref=land2.at[e], send_sem=s1b.at[src],
            recv_sem=r1b.at[e], device_id={"mem": src}, device_id_type=MESH)

    def spare_rows(dst, h):
        at = dst * H + h
        block = jnp.concatenate([prod[at][:, :Q - E], prod2[at]], axis=1).reshape(-1, L)
        return block.T.astype(jnp.bfloat16)

    if E:
        @pl.when(adopter)
        def _():
            @pl.loop(1, N)
            def _(d):
                dst = lax.rem(me + d, N)
                for h in range(H):
                    send2[dst, h] = spare_rows(dst, h)
                out1b(dst).start()

            for h in range(H):
                land2[corner, h] = spare_rows(me, h)

    def out2(kk):
        return pltpu.make_async_remote_copy(
            src_ref=land.at[pl.ds(R * kk, R)], dst_ref=o_ref.at[mk], send_sem=s2.at[kk],
            recv_sem=r2.at[mk], device_id={"ma": kk}, device_id_type=MESH)

    def in2(kk):
        return pltpu.make_async_remote_copy(
            src_ref=land.at[pl.ds(R * kk, R)], dst_ref=o_ref.at[kk], send_sem=s2.at[kk],
            recv_sem=r2.at[kk], device_id={"ma": kk}, device_id_type=MESH)

    def gather_rows(kk):
        for r in range(R):
            src = R * kk + r

            @pl.when(src != me)
            def _():
                in1(src).wait_recv()

            if E:
                low, high = src < 2, src >= N - 2
                helper = jnp.where(low, src + 2, src - 2)
                e = lax.rem(src, 2) + jnp.where(high, 2, 0)

                @pl.when(jnp.logical_and(jnp.logical_or(low, high), helper != me))
                def _():
                    in1b(e, helper).wait_recv()

                @pl.when(jnp.logical_or(low, high))
                def _():
                    lane = lax.broadcasted_iota(jnp.int32, land.shape[2:], 1)
                    spare = lane % (2 * PACK * Q) >= 2 * PACK * (Q - E)
                    for h in range(H):
                        own = land[src, h].astype(jnp.float32)
                        other = land2[e, h].astype(jnp.float32)
                        land[src, h] = jnp.where(spare, other, own).astype(jnp.bfloat16)

    for d in range(1, M):
        kk = lax.rem(mk + d, M)
        gather_rows(kk)
        out2(kk).start()
    gather_rows(mk)
    o_ref[mk] = land[pl.ds(R * mk, R)]
    for d in range(1, M):
        in2(lax.rem(mk + d, M)).wait_recv()

    @pl.loop(0, steps)
    def _(s):
        basis_copy(s).wait()

    for d in range(1, M):
        out2(lax.rem(mk + d, M)).wait_send()

    @pl.loop(1, N)
    def _(d):
        out1(lax.rem(me + d, N)).wait_send()

    @pl.loop(0, Q)
    def _(q):
        for i in range(Z):
            src = 2 * i + p
            ref = gath.at[q, src]

            @pl.when(jnp.logical_and(goes_up(q), z >= i))
            def _():
                hop(0, q, src, ref, me + 2).wait_send()

            @pl.when(jnp.logical_and(goes_down(q), z <= i))
            def _():
                hop(1, q, src, ref, me - 2).wait_send()

            @pl.when(here(q))
            def _():
                hop(2, q, src, ref, mate).wait_send()

    if E:
        @pl.when(end)
        def _():
            for e in range(E):
                adopt_copy(e).wait_send()

        @pl.when(adopter)
        def _():
            @pl.loop(1, N)
            def _(d):
                out1b(lax.rem(me + d, N)).wait_send()


def update_kernel(m_ref, d_ref, amp_ref, s_ref, f_ref, n_ref, c_ref, u_ref, v_ref, cb_ref, sb_ref, total, lons):
    step = pl.program_id(0)
    scales, members, _, _, degrees = s_ref.shape
    first = lax.axis_index("ma") * (pl.num_programs(0) * PACK) + step * PACK
    degree = lax.broadcasted_iota(jnp.int32, (2, degrees), 1)
    for j in range(PACK):
        kept = jnp.where(degree >= m_ref[first + j], 1.0, 0.0).astype(jnp.float32)
        for b in range(members):
            acc = None
            for i in range(scales):
                new = kept * (d_ref[i] * s_ref[i, b, j] + amp_ref[i:i + 1, :] * f_ref[i, b, j])
                n_ref[i, b, j] = new
                acc = new if acc is None else acc + new
            total[b * 2 * PACK + 2 * j:b * 2 * PACK + 2 * j + 2, :] = acc
    c_ref[0] = total[...].astype(jnp.bfloat16)

    unit = 2.0 * math.pi / lons
    width = u_ref.shape[1]
    group = lax.broadcasted_iota(jnp.int32, (8, 1), 0)
    shift = (group % 2).astype(jnp.float32) * (lons // 4)

    def cos_sin(x):
        x = x - lons * jnp.floor(x * (1.0 / lons) + 0.5)
        k = jnp.floor(x * (4.0 / lons) + 0.5)
        y = (x - k * (lons // 4)) * unit
        y2 = y * y
        c = 1.0 + y2 * (-1.0 / 2 + y2 * (1.0 / 24 + y2 * (-1.0 / 720 + y2 * (1.0 / 40320))))
        n = y * (1.0 + y2 * (-1.0 / 6 + y2 * (1.0 / 120 + y2 * (-1.0 / 5040 + y2 * (1.0 / 362880)))))
        odd = jnp.abs(k) == 1.0
        cos, sin = jnp.where(odd, n, c), jnp.where(odd, c, n)
        cos = jnp.where(jnp.logical_or(k >= 1.0, k <= -2.0), -cos, cos)
        sin = jnp.where(jnp.logical_or(k >= 2.0, k <= -1.0), -sin, sin)
        return cos, sin

    for g in range(u_ref.shape[0] // 8):
        at = (step * (u_ref.shape[0] // 8) + g) * PACK
        m = m_ref[at]
        near = jnp.full((8, 128), m, jnp.int32)
        far = jnp.full((8, width), lax.rem(m * 128, lons), jnp.int32)
        for j in range(1, PACK):
            m = m_ref[at + j]
            near = jnp.where(group // 2 == j, m, near)
            far = jnp.where(group // 2 == j, lax.rem(m * 128, lons), far)
        near = near * lax.broadcasted_iota(jnp.int32, (8, 128), 1)
        far = far * lax.broadcasted_iota(jnp.int32, (8, width), 1)
        cos, sin = cos_sin(far.astype(jnp.float32) + shift)
        u_ref[g * 8:(g + 1) * 8] = cos
        v_ref[g * 8:(g + 1) * 8] = -sin
        cos, sin = cos_sin(near.astype(jnp.float32))
        cb_ref[g * 8:(g + 1) * 8] = cos
        sb_ref[g * 8:(g + 1) * 8] = sin


def synth_kernel(f_ref, basis_ref, t_ref, o_ref, lhs):
    M, R, H, L, W = f_ref.shape
    half = W // 2

    @pl.when(pl.program_id(0) == 0)
    def _():
        parts = []
        for b in range(2 * H):
            for r in range(R):
                lo = (b % 2) * half
                row = [f_ref[k, r, b // 2].astype(jnp.float32)[:, lo:lo + half] for k in range(M)]
                parts.append(jnp.concatenate(row, axis=1))
        lhs[...] = jnp.concatenate(parts, axis=0).astype(jnp.bfloat16)

    pattern = jnp.dot(lhs[...], basis_ref[...], preferred_element_type=jnp.float32)
    scale = 1.0 / math.sqrt(basis_ref.shape[0] // 2)
    factor = jnp.clip(pattern * scale + 1.0, 1.0 - clip_level, 1.0 + clip_level)
    o_ref[...] = (t_ref[...].astype(jnp.float32) * factor.reshape(o_ref.shape)).astype(jnp.bfloat16)


def per_device(N, M, ar_state, forcing, ar_decay, amplitude, wavenumber, tables, tendencies):
    members, waves = ar_state.shape[1], ar_state.shape[2]
    degrees = ar_state.shape[4]
    lats = tables.shape[2]
    Q = waves // PACK
    rows = members * 2 * PACK
    scales = ar_state.shape[0]
    lons = tendencies.shape[2]
    modes = 2 * wavenumber.shape[0]
    width = -(-(lons // 128) // 128) * 128
    state_spec = pl.BlockSpec((scales, members, PACK, 2, degrees), lambda i: (0, 0, i, 0, 0))
    smem = pl.BlockSpec(memory_space=pltpu.SMEM)
    trig = lambda w: (pl.BlockSpec((modes // Q, w), lambda i: (i, 0)), jax.ShapeDtypeStruct((modes, w), jnp.float32))
    tables_out = [trig(width), trig(width), trig(128), trig(128)]
    new_state, coefficients, u, v, cb, sb = pl.pallas_call(
        functools.partial(update_kernel, lons=lons),
        grid=(Q,),
        out_shape=[
            jax.ShapeDtypeStruct(ar_state.shape, jnp.float32),
            jax.ShapeDtypeStruct((Q, rows, degrees), jnp.bfloat16),
        ] + [x[1] for x in tables_out],
        in_specs=[smem, smem, pl.BlockSpec(amplitude.shape, lambda i: (0, 0)), state_spec, state_spec],
        out_specs=[state_spec, pl.BlockSpec((1, rows, degrees), lambda i: (i, 0, 0))] + [x[0] for x in tables_out],
        scratch_shapes=[
            pltpu.VMEM((rows, degrees), jnp.float32),
        ],
        name="update",
    )(wavenumber, ar_decay, amplitude, ar_state, forcing)
    turned = tables.transpose(0, 2, 1).reshape(Q, PACK * lats, degrees)

    H = members // 2
    W = 2 * Q * 2 * PACK
    R = N // M
    any_spec = pl.BlockSpec(memory_space=pl.ANY)
    vmem_spec = pl.BlockSpec(memory_space=pltpu.VMEM)
    steps = Q + N // 2 - 2
    spare = max(tail_chunks(Q, N // 2), 1)
    cols = lons // 128 // steps
    fourier, basis = pl.pallas_call(
        functools.partial(legendre_kernel, N, M),
        out_shape=[
            jax.ShapeDtypeStruct((M, R, H, lats, W), jnp.bfloat16),
            jax.ShapeDtypeStruct((modes, lons), jnp.bfloat16),
        ],
        in_specs=[vmem_spec, any_spec] + [vmem_spec] * 4,
        out_specs=[vmem_spec, any_spec],
        scratch_shapes=[
            pltpu.VMEM((steps, modes, cols * 128), jnp.bfloat16),
            pltpu.VMEM((Q, N, rows, degrees), jnp.bfloat16),
            pltpu.VMEM((Q, PACK * lats, degrees), jnp.bfloat16),
            pltpu.VMEM((N * H, 2, Q, 2 * PACK, lats), jnp.float32),
            pltpu.VMEM((N, H, lats, W), jnp.bfloat16),
            pltpu.VMEM((N, H, lats, W), jnp.bfloat16),
            pltpu.VMEM((spare, PACK * lats, degrees), jnp.bfloat16),
            pltpu.VMEM((N * H, 2, spare, 2 * PACK, lats), jnp.float32),
            pltpu.VMEM((N, H, lats, W), jnp.bfloat16),
            pltpu.VMEM((4, H, lats, W), jnp.bfloat16),
            pltpu.SemaphoreType.DMA((steps,)),
            pltpu.SemaphoreType.DMA((Q,)),
            pltpu.SemaphoreType.DMA((Q,)),
            pltpu.SemaphoreType.DMA((3, Q, N)),
            pltpu.SemaphoreType.DMA((Q, N)),
            pltpu.SemaphoreType.DMA((N,)),
            pltpu.SemaphoreType.DMA((N,)),
            pltpu.SemaphoreType.DMA((M,)),
            pltpu.SemaphoreType.DMA((M,)),
            pltpu.SemaphoreType.DMA((spare,)),
            pltpu.SemaphoreType.DMA((spare,)),
            pltpu.SemaphoreType.DMA((N,)),
            pltpu.SemaphoreType.DMA((4,)),
        ],
        compiler_params=pltpu.CompilerParams(collective_id=0, has_side_effects=True),
        name="legendre",
    )(coefficients, turned, u, v, cb, sb)

    tile = lons // 5
    grid_spec = pl.BlockSpec((tendencies.shape[0], tendencies.shape[1], tile), lambda i: (0, 0, i))
    perturbed = pl.pallas_call(
        synth_kernel,
        grid=(lons // tile,),
        out_shape=jax.ShapeDtypeStruct(tendencies.shape, jnp.bfloat16),
        in_specs=[
            pl.BlockSpec(fourier.shape, lambda i: (0,) * 5),
            pl.BlockSpec((modes, tile), lambda i: (0, i)),
            grid_spec,
        ],
        out_specs=grid_spec,
        scratch_shapes=[pltpu.VMEM((tendencies.shape[0] * tendencies.shape[1], modes), jnp.bfloat16)],
        name="synthesis",
    )(fourier, basis, tendencies)
    return (perturbed, new_state)


def solution(mesh):
    return jax.shard_map(
        functools.partial(per_device, mesh.shape["mem"], mesh.shape["ma"]),
        mesh=mesh,
        in_specs=(
            P(None, "mem", "ma", None, None),
            P(None, "mem", "ma", None, None),
            P(),
            P(),
            P(),
            P("ma", None, "mem"),
            P("mem", "ma", None),
        ),
        out_specs=(P("mem", "ma", None), P(None, "mem", "ma", None, None)),
        check_vma=False,
    )
```
